768 devices in a mesh: dp: 48 (over z_lo, y, core), ctx: 4 (over z_hi), head: 4 (over x).
Axes of the slice: x: 4, y: 8, z: 12 (z_hi: 4, z_lo: 3; z = z_hi * 3 + z_lo), core: 2. Of those that a mesh axis runs over, the one named last changes fastest.
Arguments:
- query_long: bfloat16 [48, 512, 8192], P('dp', 'ctx', 'head'), may hold values from -6 to 6
- key_long: bfloat16 [48, 512, 1024], P('dp', 'ctx', 'head'), may hold values from -6 to 6
- long_values: bfloat16 [48, 512, 1024], P('dp', 'ctx', 'head'), may hold values from -6 to 6
- outgrad_long: bfloat16 [48, 512, 8192], P('dp', 'ctx', 'head'), may hold values from -6 to 6
- query_short: bfloat16 [48, 8, 64, 8192], P('dp', 'ctx', None, 'head'), may hold values from -6 to 6
- key_short: bfloat16 [48, 8, 64, 1024], P('dp', 'ctx', None, 'head'), may hold values from -6 to 6
- short_values: bfloat16 [48, 8, 64, 1024], P('dp', 'ctx', None, 'head'), may hold values from -6 to 6
- outgrad_short: bfloat16 [48, 8, 64, 8192], P('dp', 'ctx', None, 'head'), may hold values from -6 to 6
- segments: int32 [48, 8, 64], P('dp', 'ctx'), may hold values from 0 to 3, never falling along the last dimension, each value on 1 to 32 neighbouring positions
- assignment: int32 [48, 8], P('dp', 'ctx'), may hold values from 0 to 1, as said below
Outputs:
- output_long: bfloat16 [48, 512, 8192], P('dp', 'ctx', 'head')
- querygrad_long: bfloat16 [48, 512, 8192], P('dp', 'ctx', 'head')
- keygrad_long: bfloat16 [48, 512, 1024], P('dp', 'ctx', 'head')
- valuegrad_long: bfloat16 [48, 512, 1024], P('dp', 'ctx', 'head')
- output_short: bfloat16 [48, 8, 64, 8192], P('dp', 'ctx', None, 'head')
- querygrad_short: bfloat16 [48, 8, 64, 8192], P('dp', 'ctx', None, 'head')
- keygrad_short: bfloat16 [48, 8, 64, 1024], P('dp', 'ctx', None, 'head')
- valuegrad_short: bfloat16 [48, 8, 64, 1024], P('dp', 'ctx', None, 'head')
The draws below stay inside these ranges and needn't reach their ends.
Inputs may be any that keep to these rules, and one draw needn't show every extreme that they name: In each group of 2 tiles of a sequence (tiles c * 2 to (c + 1) * 2 - 1) exactly 1 tiles have assignment 1. `segments`: segment numbers start at 0 in each tile and never fall along it.
All inputs are finite; a program needn't handle non-finite values.
Results may differ from the reference program's by a relative error of at most 0.02.
Values may be sent and summed in bfloat16 or wider, within the bound.
No kernel may reach another device: no remote copies, remote signals or barrier semaphores. Data moves between devices by JAX's collectives and lax.ppermute only.
A program may use at most 32 MiB of HBM per device.

```python
import math
import jax
import jax.numpy as jnp
import numpy as np
from jax import lax

QUERY_HEADS = 64
KEY_VALUE_HEADS = 8
HEAD_SIZE = 128
LONG_DEV = 128
TILE_POSITIONS = 64
TILES_DEV = 2
SEGS = 4
MOVED = 1
PACKED_SEQUENCES = 48
LONG_POSITIONS = 512
SHORT_TILES = 8


def query_draw(key, leading_part):
    drawn_random_key = jax.random.fold_in(key, 11)
    return jnp.clip(jax.random.normal(drawn_random_key, leading_part + (QUERY_HEADS * HEAD_SIZE,), jnp.float32), -6.0, 6.0)


def key_draw(key, leading_part):
    drawn_random_key = jax.random.fold_in(key, 13)
    return jnp.clip(jax.random.normal(drawn_random_key, leading_part + (KEY_VALUE_HEADS * HEAD_SIZE,), jnp.float32), -6.0, 6.0)


def draw_query_long(key, part):
    return query_draw(key, (PACKED_SEQUENCES, LONG_POSITIONS)).astype(jnp.bfloat16)


def draw_key_long(key, part):
    return key_draw(key, (PACKED_SEQUENCES, LONG_POSITIONS)).astype(jnp.bfloat16)


def draw_query_short(key, part):
    return query_draw(key, (PACKED_SEQUENCES, SHORT_TILES, TILE_POSITIONS)).astype(jnp.bfloat16)


def draw_key_short(key, part):
    return key_draw(key, (PACKED_SEQUENCES, SHORT_TILES, TILE_POSITIONS)).astype(jnp.bfloat16)


def draw_assignment(key, part):
    shape = (PACKED_SEQUENCES, SHORT_TILES // TILES_DEV, TILES_DEV)
    raw_scores = jax.random.randint(key, shape, 0, 1 << 20) * TILES_DEV + lax.broadcasted_iota(jnp.int32, shape, 2)
    ranking = jnp.argsort(jnp.argsort(raw_scores, axis=-1), axis=-1)
    return (ranking < MOVED).astype(jnp.int32).reshape(PACKED_SEQUENCES, SHORT_TILES)


def block_levels(rng, shape, cuts, low, top_value):
    factor_of = 1.0
    for axis_at, blocks in cuts:
        steps = jax.random.uniform(jax.random.fold_in(jax.random.fold_in(rng, 6), axis_at), (blocks,), jnp.float32, low / len(cuts), top_value / len(cuts))
        factor_of = factor_of * jnp.repeat(jnp.exp(steps), shape[axis_at] // blocks).reshape((-1,) + (1,) * (len(shape) - 1 - axis_at))
    return factor_of


def profile(amount, total, limit, lean):
    weights = [(1 << 20) // math.isqrt(standing ** lean) + 1 for standing in range(2, amount + 1)]
    rest, counts = total - limit - (amount - 1), [1] * (amount - 1)
    while rest > 0:
        free = [i for i in range(amount - 1) if counts[i] < limit]
        mass, left = sum([weights[i] for i in free]), rest
        for i in free:
            addition = min(limit - counts[i], max(1, left * weights[i] // mass), rest)
            counts[i] = counts[i] + addition
            rest = rest - addition
    return np.array([limit] + counts)


def ragged(own_key, amount, total, reach, lean):
    if amount == 2:
        one = jax.random.randint(own_key, (), max(1, total - reach), min(reach, total - 1) + 1)
        return jnp.stack([one, total - one])
    lengths = jnp.asarray(profile(amount, total, reach, lean), jnp.int32)
    twos = (amount - 1) // 2
    donor, taker = lengths[1:1 + 2 * twos:2], lengths[2:2 + 2 * twos:2]
    slack = jnp.minimum(donor - 1, reach - taker)
    moved = jax.random.randint(jax.random.fold_in(own_key, 1), (twos,), 0, 1 << 20) % (slack + 1)
    lengths = lengths.at[1:1 + 2 * twos:2].set(donor - moved).at[2:2 + 2 * twos:2].set(taker + moved)
    return lengths[jax.random.permutation(jax.random.fold_in(own_key, 2), amount)]


def gaussian(rng, dims, scale, limit, split=(), dtype=jnp.bfloat16):
    factor_of = block_levels(rng, dims, split, -0.22, 0.18) if split else 1.0
    values = jax.random.normal(rng, dims, jnp.float32) * scale * factor_of
    return jnp.minimum(jnp.maximum(values, -limit), limit).astype(dtype)


def setup_inputs(seed: int = 0) -> dict:
    splits = jax.random.split(jax.random.key(seed), 11)
    return {
        "query_long": draw_query_long(jax.random.fold_in(splits[10], 71), 0),
        "key_long": draw_key_long(jax.random.fold_in(splits[10], 71), 0),
        "long_values": gaussian(splits[2], (PACKED_SEQUENCES, LONG_POSITIONS, KEY_VALUE_HEADS * HEAD_SIZE), 1.0, 6.0, ((0, 48), (1, 4), (2, 4))),
        "outgrad_long": gaussian(splits[3], (PACKED_SEQUENCES, LONG_POSITIONS, QUERY_HEADS * HEAD_SIZE), 1.0, 6.0, ((0, 48), (1, 4), (2, 4))),
        "query_short": draw_query_short(jax.random.fold_in(splits[10], 71), 0),
        "key_short": draw_key_short(jax.random.fold_in(splits[10], 71), 0),
        "short_values": gaussian(splits[6], (PACKED_SEQUENCES, SHORT_TILES, TILE_POSITIONS, KEY_VALUE_HEADS * HEAD_SIZE), 1.0, 6.0, ((0, 48), (1, 4), (3, 4))),
        "outgrad_short": gaussian(splits[7], (PACKED_SEQUENCES, SHORT_TILES, TILE_POSITIONS, QUERY_HEADS * HEAD_SIZE), 1.0, 6.0, ((0, 48), (1, 4), (3, 4))),
        "segments": jax.vmap(lambda own: jnp.searchsorted(jnp.cumsum(ragged(own, SEGS, TILE_POSITIONS, TILE_POSITIONS // 2, 2)), jnp.arange(TILE_POSITIONS), side="right"))(jax.random.split(splits[8], PACKED_SEQUENCES * SHORT_TILES)).reshape((PACKED_SEQUENCES, SHORT_TILES, TILE_POSITIONS)).astype(jnp.int32),
        "assignment": draw_assignment(jax.random.fold_in(splits[10], 71), 0),
    }


def attend(queries, key_rows, value_rows, out_grad, allowed):
    rows = queries.shape[0]
    cols = key_rows.shape[0]
    kv_heads = key_rows.shape[1] // HEAD_SIZE
    query_group = queries.shape[1] // key_rows.shape[1]
    scaling = 1.0 / math.sqrt(HEAD_SIZE)
    float_query = queries.astype(jnp.float32).reshape(rows, kv_heads, query_group, HEAD_SIZE)
    float_key = key_rows.astype(jnp.float32).reshape(cols, kv_heads, HEAD_SIZE)
    float_value = value_rows.astype(jnp.float32).reshape(cols, kv_heads, HEAD_SIZE)
    float_grad = out_grad.astype(jnp.float32).reshape(rows, kv_heads, query_group, HEAD_SIZE)
    scores = jnp.einsum('rhgd,chd->hgrc', float_query, float_key) * scaling
    scores = jnp.where(allowed[None, None], scores, -jnp.inf)
    row_max = lax.optimization_barrier(jnp.max(scores, axis=-1, keepdims=True))
    log_total = row_max + jnp.log(lax.optimization_barrier(jnp.sum(jnp.exp(scores - row_max), axis=-1, keepdims=True)))
    weights = jnp.exp(scores - log_total)
    weights_half = weights.astype(jnp.bfloat16).astype(jnp.float32)
    output = jnp.einsum('hgrc,chd->rhgd', weights_half, float_value).astype(jnp.bfloat16)
    row_dots = lax.optimization_barrier(jnp.sum(float_grad * output.astype(jnp.float32), axis=-1))
    row_dots = jnp.transpose(row_dots, (1, 2, 0))[..., None]
    weight_grad = jnp.einsum('rhgd,chd->hgrc', float_grad, float_value)
    score_grad = (weights * (weight_grad - row_dots)).astype(jnp.bfloat16).astype(jnp.float32)
    querygrad = (jnp.einsum('hgrc,chd->rhgd', score_grad, float_key) * scaling).astype(jnp.bfloat16)
    keygrad = jnp.einsum('hgrc,rhgd->chd', score_grad, float_query) * scaling
    valuegrad = jnp.einsum('hgrc,rhgd->chd', weights_half, float_grad)
    return (output.reshape(rows, -1), querygrad.reshape(rows, -1), keygrad.reshape(cols, -1), valuegrad.reshape(cols, -1))

def long_sequence(items):
    queries, key_rows, value_rows, out_grad = items
    key_pos = lax.iota(jnp.int32, LONG_POSITIONS)
    outputs = []
    querygrads = []
    key_sum = jnp.zeros(key_rows.shape, jnp.float32)
    value_sum = jnp.zeros(value_rows.shape, jnp.float32)
    for block in range(LONG_POSITIONS // LONG_DEV):
        first = block * LONG_DEV
        query_pos = first + lax.iota(jnp.int32, LONG_DEV)
        allowed = key_pos[None, :] <= query_pos[:, None]
        output, querygrad, keygrad, valuegrad = attend(queries[first:first + LONG_DEV], key_rows, value_rows, out_grad[first:first + LONG_DEV], allowed)
        outputs.append(output)
        querygrads.append(querygrad)
        key_sum = key_sum + keygrad.astype(jnp.bfloat16).astype(jnp.float32)
        value_sum = value_sum + valuegrad.astype(jnp.bfloat16).astype(jnp.float32)
    return (jnp.concatenate(outputs, axis=0), jnp.concatenate(querygrads, axis=0), key_sum.astype(jnp.bfloat16), value_sum.astype(jnp.bfloat16))

def short_tile(items):
    queries, key_rows, value_rows, out_grad, labels = items
    position = lax.iota(jnp.int32, TILE_POSITIONS)
    allowed = (labels[None, :] == labels[:, None]) & (position[None, :] <= position[:, None])
    output, querygrad, keygrad, valuegrad = attend(queries, key_rows, value_rows, out_grad, allowed)
    return (output, querygrad, keygrad.astype(jnp.bfloat16), valuegrad.astype(jnp.bfloat16))

def relayout(tiles_flat, assignment):
    groups = SHORT_TILES // TILES_DEV
    flags = assignment.reshape(PACKED_SEQUENCES, groups, TILES_DEV)
    order = jnp.argsort(flags, axis=-1, stable=True).astype(jnp.int32)
    kept = order[..., :TILES_DEV - MOVED]
    sent = order[..., TILES_DEV - MOVED:]
    seq_index = lax.broadcasted_iota(jnp.int32, (PACKED_SEQUENCES, groups, 1), 0)
    group_index = lax.broadcasted_iota(jnp.int32, (PACKED_SEQUENCES, groups, 1), 1)
    own = seq_index * SHORT_TILES + group_index * TILES_DEV + kept
    arrived = (seq_index - 1) % PACKED_SEQUENCES * SHORT_TILES + group_index * TILES_DEV + jnp.roll(sent, 1, axis=0)
    picked = jnp.concatenate([own, arrived], axis=-1).reshape(-1).astype(jnp.int32)
    return tiles_flat[picked].reshape(PACKED_SEQUENCES, SHORT_TILES, TILE_POSITIONS, -1)

def reference(query_long, key_long, long_values, outgrad_long, query_short, key_short, short_values, outgrad_short, segments, assignment):
    output_long, querygrad_long, keygrad_long, valuegrad_long = lax.map(long_sequence, (query_long, key_long, long_values, outgrad_long))
    count = PACKED_SEQUENCES * SHORT_TILES
    flat = (query_short.reshape(count, TILE_POSITIONS, -1), key_short.reshape(count, TILE_POSITIONS, -1), short_values.reshape(count, TILE_POSITIONS, -1), outgrad_short.reshape(count, TILE_POSITIONS, -1), segments.reshape(count, TILE_POSITIONS))
    output_tiles, querygrad_tiles, keygrad_tiles, valuegrad_tiles = lax.map(short_tile, flat)
    return (output_long, querygrad_long, keygrad_long, valuegrad_long, relayout(output_tiles, assignment), relayout(querygrad_tiles, assignment), relayout(keygrad_tiles, assignment), relayout(valuegrad_tiles, assignment))
```

```python
import math

import jax
import jax.numpy as jnp
from jax import lax
from jax.experimental import pallas as pl
from jax.experimental.pallas import tpu as pltpu
from jax.sharding import PartitionSpec as P

HEAD = 128
SCALE = 1.0 / math.sqrt(HEAD)
EXP2_SCALE = SCALE / math.log(2.0)
MASKED = -1e30
F32 = jnp.float32
BF16 = jnp.bfloat16


def dot_nt(a, b):
    return lax.dot_general(a, b, (((1,), (1,)), ((), ())), preferred_element_type=F32)


def dot_nn(a, b):
    return jnp.dot(a, b, preferred_element_type=F32)


def dot_tn(a, b):
    return lax.dot_general(a, b, (((0,), (0,)), ((), ())), preferred_element_type=F32)


def attend(q, g, k, v, bias):
    raw = dot_nt(q, k) + bias
    top = jnp.max(raw, axis=-1, keepdims=True)
    grown = jnp.exp2((raw - top) * EXP2_SCALE)
    weights = grown * (1.0 / jnp.sum(grown, axis=-1, keepdims=True))
    half = weights.astype(BF16)
    out = dot_nn(half, v).astype(BF16)
    weight_grad = dot_nt(g, v)
    row_dots = jnp.sum(g.astype(F32) * out.astype(F32), axis=-1, keepdims=True)
    score_grad = (weights * (weight_grad - row_dots)).astype(BF16)
    q_grad = (dot_nn(score_grad, k) * SCALE).astype(BF16)
    return half, score_grad, out, q_grad


def heads_of(ref, first, count, rows):
    return jnp.concatenate(
        [ref[rows, (first + j) * HEAD:(first + j + 1) * HEAD] for j in range(count)], axis=0
    )


def pack_kv(k_ref, v_ref, o_ref):
    o_ref[:, :256] = k_ref[...]
    o_ref[:, 256:] = v_ref[...]


def pack_tile(where_ref, q_ref, g_ref, k_ref, v_ref, seg_ref, o_ref):
    at = 1 - where_ref[0, 0]
    o_ref[:, 0:2048] = q_ref[0]
    o_ref[:, 2048:4096] = g_ref[0]
    o_ref[:, 4096:4352] = k_ref[0]
    o_ref[:, 4352:4608] = v_ref[0]
    labels = seg_ref[pl.ds(at, 1), :].astype(F32)
    plane = jnp.concatenate([labels, jnp.zeros_like(labels)], axis=1)
    o_ref[:, 4608:4736] = jnp.broadcast_to(plane, (64, 128)).astype(BF16)


def long_kernel(q_ref, g_ref, own_k, own_v, one_ref, two_ref, three_ref,
                out_ref, qg_ref, own_o, one_o, two_o, three_o, *, group):
    place = lax.axis_index("ctx")
    rows = q_ref.shape[0]
    shape = (rows, 4 * rows)
    col = lax.broadcasted_iota(jnp.int32, shape, 1)
    row = lax.broadcasted_iota(jnp.int32, shape, 0)
    allowed = ((col < rows) & (col <= row)) | ((col >= rows) & (col < (place + 1) * rows))
    bias = jnp.where(allowed, 0.0, MASKED).astype(F32)
    bias = jnp.concatenate([bias] * group, axis=0)
    for h in range(2):
        ks = slice(h * HEAD, (h + 1) * HEAD)
        vs = slice(256 + h * HEAD, 256 + (h + 1) * HEAD)
        k = jnp.concatenate([own_k[:, ks], one_ref[:, ks], two_ref[:, ks], three_ref[:, ks]], axis=0)
        v = jnp.concatenate([own_v[:, ks], one_ref[:, vs], two_ref[:, vs], three_ref[:, vs]], axis=0)
        k_sum = jnp.zeros((HEAD, 4 * rows), F32)
        v_sum = jnp.zeros((HEAD, 4 * rows), F32)
        for first in range(h * 8, h * 8 + 8, group):
            q = heads_of(q_ref, first, group, slice(None))
            g = heads_of(g_ref, first, group, slice(None))
            half, score_grad, out, q_grad = attend(q, g, k, v, bias)
            for j in range(group):
                at = slice((first + j) * HEAD, (first + j + 1) * HEAD)
                out_ref[:, at] = out[j * rows:(j + 1) * rows]
                qg_ref[:, at] = q_grad[j * rows:(j + 1) * rows]
            k_sum = k_sum + dot_tn(q, score_grad)
            v_sum = v_sum + dot_tn(g, half)
        k_grad = jnp.transpose(k_sum * SCALE).astype(BF16)
        v_grad = jnp.transpose(v_sum).astype(BF16)
        for i, ref in enumerate((own_o, one_o, two_o, three_o)):
            ref[:, ks] = k_grad[i * rows:(i + 1) * rows]
            ref[:, vs] = v_grad[i * rows:(i + 1) * rows]


def tile_work(q_ref, g_ref, k_ref, v_ref, labels, store):
    rows = 64
    seen = lax.broadcasted_iota(jnp.int32, (8, rows), 0).astype(F32)
    onehot = (seen == jnp.broadcast_to(labels, (8, rows))).astype(F32)
    same = dot_tn(onehot, onehot)
    col = lax.broadcasted_iota(jnp.int32, (rows, rows), 1)
    row = lax.broadcasted_iota(jnp.int32, (rows, rows), 0)
    bias = jnp.where((same > 0.5) & (col <= row), 0.0, MASKED).astype(F32)
    bias = jnp.concatenate([bias] * 8, axis=0)
    for h in range(2):
        ks = slice(h * HEAD, (h + 1) * HEAD)
        k, v = k_ref[:, ks], v_ref[:, ks]
        q = heads_of(q_ref, h * 8, 8, slice(None))
        g = heads_of(g_ref, h * 8, 8, slice(None))
        half, score_grad, out, q_grad = attend(q, g, k, v, bias)
        k_grad = (dot_tn(score_grad, q) * SCALE).astype(BF16)
        v_grad = dot_tn(half, g).astype(BF16)
        store(h, out, q_grad, k_grad, v_grad)


def store_tile(out_ref, qg_ref, kg_ref, vg_ref, h, out, q_grad, k_grad, v_grad):
    for j in range(8):
        at = slice((h * 8 + j) * HEAD, (h * 8 + j + 1) * HEAD)
        out_ref[0, :, at] = out[j * 64:(j + 1) * 64]
        qg_ref[0, :, at] = q_grad[j * 64:(j + 1) * 64]
    ks = slice(h * HEAD, (h + 1) * HEAD)
    kg_ref[0, :, ks] = k_grad
    vg_ref[0, :, ks] = v_grad


def kept_kernel(where_ref, q_ref, g_ref, k_ref, v_ref, seg_ref, out_ref, qg_ref, kg_ref, vg_ref):
    labels = seg_ref[pl.ds(where_ref[0, 0], 1), :].astype(F32)

    def store(*results):
        store_tile(out_ref, qg_ref, kg_ref, vg_ref, *results)

    tile_work(q_ref.at[0], g_ref.at[0], k_ref.at[0], v_ref.at[0], labels, store)


def moved_kernel(pack_ref, a, b, c, d, out_ref, qg_ref, kg_ref, vg_ref):
    labels = pack_ref[0:1, 4608:4672].astype(F32)

    def store(*results):
        store_tile(out_ref, qg_ref, kg_ref, vg_ref, *results)

    tile_work(
        pack_ref.at[:, 0:2048], pack_ref.at[:, 2048:4096], pack_ref.at[:, 4096:4352],
        pack_ref.at[:, 4352:4608], labels, store,
    )


def finish(own, one, two, three, k_ref, v_ref):
    total = own[...].astype(F32) + one[...].astype(F32) + two[...].astype(F32) + three[...].astype(F32)
    k_ref[...] = total[:, :256].astype(BF16)
    v_ref[...] = total[:, 256:].astype(BF16)


def shaped(*shape):
    return jax.ShapeDtypeStruct(shape, BF16)


def cost(flops, moved, exps):
    return pl.CostEstimate(flops=flops, bytes_accessed=moved, transcendentals=exps)


def send(value, axis, pairs):
    return lax.ppermute(value, axis, pairs)


def local(query_long, key_long, long_values, outgrad_long, query_short, key_short,
          short_values, outgrad_short, segments, assignment):
    kv = pl.pallas_call(
        pack_kv, out_shape=shaped(128, 512), name="pack_kv",
        cost_estimate=cost(0, 1 << 18, 0),
    )(key_long[0], long_values[0])
    size = lax.axis_size("ctx")
    behind = [
        send(kv, "ctx", [(c, c + step) for c in range(size - step)]) for step in (1, 2, 3)
    ]

    short = (query_short[0], outgrad_short[0], key_short[0], short_values[0])
    widths = (2048, 2048, 256, 256)
    seg_spec = pl.BlockSpec((2, 64), lambda i, where: (0, 0))
    pack = pl.pallas_call(
        pack_tile,
        grid_spec=pltpu.PrefetchScalarGridSpec(
            num_scalar_prefetch=1, grid=(1,),
            in_specs=[pl.BlockSpec((1, 64, w), lambda i, where: (1 - where[0, 0], 0, 0)) for w in widths]
            + [seg_spec],
            out_specs=pl.BlockSpec((64, 4736), lambda i, where: (0, 0)),
        ),
        out_shape=shaped(64, 4736), name="pack_tile",
        cost_estimate=cost(0, 1 << 20, 0),
    )(assignment, *short, segments[0])
    count = lax.axis_size("dp")
    arrived = send(pack, "dp", [(c, (c + 1) % count) for c in range(count)])

    tile_cost = cost(2 * 6 * 16 * 64 * 64 * 128, 1 << 20, 16 * 64 * 64)
    tile_shapes = [shaped(2, 64, w) for w in widths]
    kept = pl.pallas_call(
        kept_kernel,
        grid_spec=pltpu.PrefetchScalarGridSpec(
            num_scalar_prefetch=1, grid=(1,),
            in_specs=[pl.BlockSpec((1, 64, w), lambda i, where: (where[0, 0], 0, 0)) for w in widths]
            + [seg_spec],
            out_specs=[pl.BlockSpec((1, 64, w), lambda i, where: (0, 0, 0)) for w in widths],
        ),
        out_shape=tile_shapes, name="kept_tile",
        cost_estimate=tile_cost,
    )(assignment, *short, segments[0])

    rows = query_long.shape[1]
    results = pl.pallas_call(
        lambda *refs: long_kernel(*refs, group=2),
        out_shape=[shaped(rows, 2048), shaped(rows, 2048)] + [shaped(rows, 512)] * 4,
        name="long_block",
        cost_estimate=cost(2 * 6 * 16 * 128 * 512 * 128, 3 << 20, 16 * 128 * 512),
    )(query_long[0], outgrad_long[0], key_long[0], long_values[0], *behind)
    output, querygrad, own = results[:3]
    parts = [
        send(part, "ctx", [(c, c - step) for c in range(step, size)])
        for step, part in zip((1, 2, 3), results[3:])
    ]

    tiles = pl.pallas_call(
        moved_kernel,
        grid=(1,),
        in_specs=[pl.BlockSpec((64, 4736), lambda i: (0, 0))]
        + [pl.BlockSpec(memory_space=pl.ANY)] * 4,
        out_specs=[pl.BlockSpec((1, 64, w), lambda i: (1, 0, 0)) for w in widths],
        out_shape=tile_shapes, name="moved_tile",
        input_output_aliases={1: 0, 2: 1, 3: 2, 4: 3},
        cost_estimate=tile_cost,
    )(arrived, *kept)

    key_sum, value_sum = pl.pallas_call(
        finish, out_shape=[shaped(rows, 256)] * 2, name="finish",
        cost_estimate=cost(1 << 18, 1 << 19, 0),
    )(own, *parts)
    return (
        output[None], querygrad[None], key_sum[None], value_sum[None],
        tiles[0][None], tiles[1][None], tiles[2][None], tiles[3][None],
    )


def solution(mesh):
    long_spec = P("dp", "ctx", "head")
    tile_spec = P("dp", "ctx", None, "head")
    return jax.shard_map(
        local, mesh=mesh,
        in_specs=(long_spec,) * 4 + (tile_spec,) * 4 + (P("dp", "ctx", None), P("dp", "ctx")),
        out_specs=(long_spec,) * 4 + (tile_spec,) * 4,
        check_vma=False,
    )
```

```python
import math

import jax
import jax.numpy as jnp
from jax import lax
from jax.experimental import pallas as pl
from jax.experimental.pallas import tpu as pltpu
from jax.sharding import PartitionSpec as P


HEAD = 128
SCALE = 1.0 / math.sqrt(HEAD)
EXP2_SCALE = SCALE / math.log(2.0)
MASKED = -1e30
GROUP = 8
F32 = jnp.float32
BF16 = jnp.bfloat16


def dot_nt(a, b):
    return lax.dot_general(a, b, (((1,), (1,)), ((), ())), preferred_element_type=F32)


def dot_nn(a, b):
    return jnp.dot(a, b, preferred_element_type=F32)


def dot_tn(a, b):
    return lax.dot_general(a, b, (((0,), (0,)), ((), ())), preferred_element_type=F32)


def attend(q, g, k, v, bias):
    raw = dot_nt(q, k) + bias
    top = jnp.max(raw, axis=-1, keepdims=True)
    grown = jnp.exp2((raw - top) * EXP2_SCALE)
    weights = grown * (1.0 / jnp.sum(grown, axis=-1, keepdims=True))
    half = weights.astype(BF16)
    out = dot_nn(half, v).astype(BF16)
    weight_grad = dot_nt(g, v)
    row_dots = jnp.sum(g.astype(F32) * out.astype(F32), axis=-1, keepdims=True)
    score_grad = (weights * (weight_grad - row_dots)).astype(BF16)
    q_grad = (dot_nn(score_grad, k) * SCALE).astype(BF16)
    return half, score_grad, out, q_grad


def heads_of(ref, first, count, rows):
    return jnp.concatenate(
        [ref[rows, (first + j) * HEAD:(first + j + 1) * HEAD] for j in range(count)], axis=0
    )


def pack_tile(where_ref, q_ref, g_ref, k_ref, v_ref, seg_ref, o_ref):
    at = 1 - where_ref[0, 0]
    o_ref[:, 0:2048] = q_ref[0]
    o_ref[:, 2048:4096] = g_ref[0]
    o_ref[:, 4096:4352] = k_ref[0]
    o_ref[:, 4352:4608] = v_ref[0]
    labels = seg_ref[pl.ds(at, 1), :].astype(F32)
    plane = jnp.concatenate([labels, jnp.zeros_like(labels)], axis=1)
    o_ref[:, 4608:4736] = jnp.broadcast_to(plane, (64, 128)).astype(BF16)


def long_head(q_ref, g_ref, own_ref, near_one, near_two, far_one, far_two, far_three, *rest, head, group):
    out_ref, qg_ref, own_o, one_o, two_o, three_o = rest[-6:]
    place = lax.axis_index("ctx")
    rows = q_ref.shape[0]
    shape = (rows, 4 * rows)
    col = lax.broadcasted_iota(jnp.int32, shape, 1)
    row = lax.broadcasted_iota(jnp.int32, shape, 0)
    allowed = ((col < rows) & (col <= row)) | ((col >= rows) & (col < (place + 1) * rows))
    bias = jnp.where(allowed, 0.0, MASKED).astype(F32)
    bias = jnp.concatenate([bias] * group, axis=0)

    def keys_of(first):
        at = slice(first + head * HEAD, first + (head + 1) * HEAD)
        return jnp.concatenate([
            own_ref[:, at], near_one[:, at] + far_one[:, at], near_two[:, at] + far_two[:, at], far_three[:, at],
        ], axis=0)

    k, v = keys_of(0), keys_of(2 * HEAD)
    k_sum = jnp.zeros((HEAD, 4 * rows), F32)
    v_sum = jnp.zeros((HEAD, 4 * rows), F32)
    for first in range(0, 8, group):
        q = heads_of(q_ref, first, group, slice(None))
        g = heads_of(g_ref, first, group, slice(None))
        half, score_grad, out, q_grad = attend(q, g, k, v, bias)
        for j in range(group):
            at = slice((first + j) * HEAD, (first + j + 1) * HEAD)
            out_ref[:, at] = out[j * rows:(j + 1) * rows]
            qg_ref[:, at] = q_grad[j * rows:(j + 1) * rows]
        k_sum = k_sum + dot_tn(q, score_grad)
        v_sum = v_sum + dot_tn(g, half)
    k_grad = jnp.transpose(k_sum * SCALE).astype(BF16)
    v_grad = jnp.transpose(v_sum).astype(BF16)
    for i, ref in enumerate((own_o, one_o, two_o, three_o)):
        ref[:, :HEAD] = k_grad[i * rows:(i + 1) * rows]
        ref[:, HEAD:] = v_grad[i * rows:(i + 1) * rows]


def tile_work(q_ref, g_ref, k_ref, v_ref, labels, store):
    rows = 64
    seen = lax.broadcasted_iota(jnp.int32, (8, rows), 0).astype(F32)
    onehot = (seen == jnp.broadcast_to(labels, (8, rows))).astype(F32)
    same = dot_tn(onehot, onehot)
    col = lax.broadcasted_iota(jnp.int32, (rows, rows), 1)
    row = lax.broadcasted_iota(jnp.int32, (rows, rows), 0)
    bias = jnp.where((same > 0.5) & (col <= row), 0.0, MASKED).astype(F32)
    bias = jnp.concatenate([bias] * 8, axis=0)
    for h in range(2):
        ks = slice(h * HEAD, (h + 1) * HEAD)
        k, v = k_ref[:, ks], v_ref[:, ks]
        q = heads_of(q_ref, h * 8, 8, slice(None))
        g = heads_of(g_ref, h * 8, 8, slice(None))
        half, score_grad, out, q_grad = attend(q, g, k, v, bias)
        k_grad = (dot_tn(score_grad, q) * SCALE).astype(BF16)
        v_grad = dot_tn(half, g).astype(BF16)
        store(h, out, q_grad, k_grad, v_grad)


def store_tile(out_ref, qg_ref, kg_ref, vg_ref, h, out, q_grad, k_grad, v_grad):
    for j in range(8):
        at = slice((h * 8 + j) * HEAD, (h * 8 + j + 1) * HEAD)
        out_ref[0, :, at] = out[j * 64:(j + 1) * 64]
        qg_ref[0, :, at] = q_grad[j * 64:(j + 1) * 64]
    ks = slice(h * HEAD, (h + 1) * HEAD)
    kg_ref[0, :, ks] = k_grad
    vg_ref[0, :, ks] = v_grad


def kept_kernel(where_ref, q_ref, g_ref, k_ref, v_ref, seg_ref, out_ref, qg_ref, kg_ref, vg_ref):
    labels = seg_ref[pl.ds(where_ref[0, 0], 1), :].astype(F32)

    def store(*results):
        store_tile(out_ref, qg_ref, kg_ref, vg_ref, *results)

    tile_work(q_ref.at[0], g_ref.at[0], k_ref.at[0], v_ref.at[0], labels, store)


def moved_kernel(early_ref, late_ref, a, b, c, d, out_ref, qg_ref, kg_ref, vg_ref, pack_ref):
    pack_ref[...] = early_ref[...] + late_ref[...]
    labels = pack_ref[0:1, 4608:4672].astype(F32)

    def store(*results):
        store_tile(out_ref, qg_ref, kg_ref, vg_ref, *results)

    tile_work(
        pack_ref.at[:, 0:2048], pack_ref.at[:, 2048:4096], pack_ref.at[:, 4096:4352],
        pack_ref.at[:, 4352:4608], labels, store,
    )


def finish(*refs):
    k_ref, v_ref = refs[-2:]
    for h in range(2):
        total = sum(ref[...].astype(F32) for ref in refs[4 * h:4 * h + 4])
        at = slice(h * HEAD, (h + 1) * HEAD)
        k_ref[:, at] = total[:, :HEAD].astype(BF16)
        v_ref[:, at] = total[:, HEAD:].astype(BF16)


def shaped(*shape):
    return jax.ShapeDtypeStruct(shape, BF16)


def cost(flops, moved, exps):
    return pl.CostEstimate(flops=flops, bytes_accessed=moved, transcendentals=exps)


def grant(mib):
    return pltpu.CompilerParams(vmem_limit_bytes=mib << 20)


def work(query_long, key_long, long_values, outgrad_long, query_short, key_short,
         short_values, outgrad_short, segments, assignment):
    rows = query_long.shape[1]
    size = lax.axis_size("ctx")
    whole = pl.BlockSpec(memory_space=pltpu.VMEM)
    packed = jnp.concatenate([key_long[0], long_values[0]], axis=1)
    last = size - 1
    near = [lax.ppermute(packed, "ctx", [(c, c + step) for c in range(last - step)]) for step in (1, 2)]
    far = [lax.ppermute(packed, "ctx", [(last - step, last)]) for step in (1, 2, 3)]

    short = (query_short[0], outgrad_short[0], key_short[0], short_values[0])
    widths = (2048, 2048, 256, 256)
    seg_spec = pl.BlockSpec((2, 64), lambda i, where: (0, 0))
    pack = pl.pallas_call(
        pack_tile,
        grid_spec=pltpu.PrefetchScalarGridSpec(
            num_scalar_prefetch=1, grid=(1,),
            in_specs=[pl.BlockSpec((1, 64, w), lambda i, where: (1 - where[0, 0], 0, 0)) for w in widths]
            + [seg_spec],
            out_specs=pl.BlockSpec((64, 4736), lambda i, where: (0, 0)),
        ),
        out_shape=shaped(64, 4736), name="pack_tile",
        cost_estimate=cost(0, 1 << 20, 0), compiler_params=grant(6),
    )(assignment, *short, segments[0])
    count = lax.axis_size("dp")
    pairs = [
        (source * size + c, (source + 1) % count * size + c) for source in range(count) for c in range(size)
    ]
    late = [((count - 1) * size, 0)]
    early = [pair for pair in pairs if pair not in late]
    arrived = lax.ppermute(pack, ("dp", "ctx"), early)
    arrived_late = lax.ppermute(pack, ("dp", "ctx"), late)

    tile_cost = cost(2 * 6 * 16 * 64 * 64 * 128, 1 << 20, 16 * 64 * 64)
    tile_shapes = [shaped(2, 64, w) for w in widths]
    kept = pl.pallas_call(
        kept_kernel,
        grid_spec=pltpu.PrefetchScalarGridSpec(
            num_scalar_prefetch=1, grid=(1,),
            in_specs=[pl.BlockSpec((1, 64, w), lambda i, where: (where[0, 0], 0, 0)) for w in widths]
            + [seg_spec],
            out_specs=[pl.BlockSpec((1, 64, w), lambda i, where: (0, 0, 0)) for w in widths],
        ),
        out_shape=tile_shapes, name="kept_tile",
        cost_estimate=tile_cost, compiler_params=grant(16),
    )(assignment, *short, segments[0])

    wide = [shaped(rows, 2048), shaped(rows, 2048)]
    done = []
    parts = []
    for h in range(2):
        half_spec = pl.BlockSpec((rows, 1024), lambda i, h=h: (0, h))
        results = pl.pallas_call(
            lambda *refs, h=h: long_head(*refs, head=h, group=GROUP),
            grid=(1,),
            in_specs=[half_spec, half_spec] + [whole] * 6
            + [pl.BlockSpec(memory_space=pl.ANY)] * len(done),
            out_specs=[half_spec, half_spec] + [whole] * 4,
            out_shape=wide + [shaped(rows, 256)] * 4,
            input_output_aliases={8: 0, 9: 1} if done else {},
            cost_estimate=cost(6 * 8 * 128 * 512 * 128, 3 << 19, 8 * 128 * 512),
            compiler_params=grant(24),
        )(query_long[0], outgrad_long[0], packed, *near, *far, *done)
        done = results[:2]
        parts += [results[2]] + [
            lax.ppermute(part, "ctx", [(c, c - step) for c in range(step, size)])
            for step, part in zip((1, 2, 3), results[3:])
        ]

    tiles = pl.pallas_call(
        moved_kernel,
        grid=(1,),
        in_specs=[whole] * 2
        + [pl.BlockSpec(memory_space=pl.ANY)] * 4,
        out_specs=[pl.BlockSpec((1, 64, w), lambda i: (1, 0, 0)) for w in widths],
        out_shape=tile_shapes, name="moved_tile",
        input_output_aliases={2: 0, 3: 1, 4: 2, 5: 3},
        scratch_shapes=[pltpu.VMEM((64, 4736), BF16)],
        cost_estimate=tile_cost, compiler_params=grant(16),
    )(arrived, arrived_late, *kept)

    key_sum, value_sum = pl.pallas_call(
        finish, out_shape=[shaped(rows, 256)] * 2, name="finish",
        cost_estimate=cost(1 << 18, 1 << 19, 0), compiler_params=grant(4),
    )(*parts)
    return (
        done[0][None], done[1][None], key_sum[None], value_sum[None],
        tiles[0][None], tiles[1][None], tiles[2][None], tiles[3][None],
    )


def solution(mesh):
    long_spec = P("dp", "ctx", "head")
    tile_spec = P("dp", "ctx", None, "head")
    return jax.shard_map(
        work, mesh=mesh,
        in_specs=(long_spec,) * 4 + (tile_spec,) * 4 + (P("dp", "ctx", None), P("dp", "ctx")),
        out_specs=(long_spec,) * 4 + (tile_spec,) * 4,
        check_vma=False,
    )
```

```python
import math

import jax
import jax.numpy as jnp
from jax import lax
from jax.experimental import pallas as pl
from jax.experimental.pallas import tpu as pltpu
from jax.sharding import PartitionSpec as P


HEAD = 128
SCALE = 1.0 / math.sqrt(HEAD)
EXP2_SCALE = SCALE / math.log(2.0)
MASKED = -1e30
GROUP = 8
F32 = jnp.float32
BF16 = jnp.bfloat16


def dot_nt(a, b):
    return lax.dot_general(a, b, (((1,), (1,)), ((), ())), preferred_element_type=F32)


def dot_nn(a, b):
    return jnp.dot(a, b, preferred_element_type=F32)


def dot_tn(a, b):
    return lax.dot_general(a, b, (((0,), (0,)), ((), ())), preferred_element_type=F32)


def attend(q, g, k, v, bias):
    raw = dot_nt(q, k) + bias
    top = jnp.max(raw, axis=-1, keepdims=True)
    grown = jnp.exp2((raw - top) * EXP2_SCALE)
    weights = grown * (1.0 / jnp.sum(grown, axis=-1, keepdims=True))
    half = weights.astype(BF16)
    out = dot_nn(half, v).astype(BF16)
    weight_grad = dot_nt(g, v)
    row_dots = jnp.sum(g.astype(F32) * out.astype(F32), axis=-1, keepdims=True)
    score_grad = (weights * (weight_grad - row_dots)).astype(BF16)
    q_grad = (dot_nn(score_grad, k) * SCALE).astype(BF16)
    return half, score_grad, out, q_grad


def heads_of(ref, first, count, rows):
    return jnp.concatenate(
        [ref[rows, (first + j) * HEAD:(first + j + 1) * HEAD] for j in range(count)], axis=0
    )


def pack_tile(where_ref, q_ref, g_ref, k_ref, v_ref, seg_ref, o_ref):
    at = 1 - where_ref[0, 0]
    o_ref[:, 0:2048] = q_ref[0]
    o_ref[:, 2048:4096] = g_ref[0]
    o_ref[:, 4096:4352] = k_ref[0]
    o_ref[:, 4352:4608] = v_ref[0]
    labels = seg_ref[pl.ds(at, 1), :].astype(F32)
    plane = jnp.concatenate([labels, jnp.zeros_like(labels)], axis=1)
    o_ref[:, 4608:4736] = jnp.broadcast_to(plane, (64, 128)).astype(BF16)


def long_head(q_ref, g_ref, own_ref, near_one, near_two, far_one, far_two, far_three, *rest, head, group):
    out_ref, qg_ref, own_o, one_o, two_o, three_o = rest[-6:]
    place = lax.axis_index("ctx")
    rows = q_ref.shape[0]
    shape = (rows, 4 * rows)
    col = lax.broadcasted_iota(jnp.int32, shape, 1)
    row = lax.broadcasted_iota(jnp.int32, shape, 0)
    allowed = ((col < rows) & (col <= row)) | ((col >= rows) & (col < (place + 1) * rows))
    bias = jnp.where(allowed, 0.0, MASKED).astype(F32)
    bias = jnp.concatenate([bias] * group, axis=0)

    def keys_of(first):
        at = slice(first + head * HEAD, first + (head + 1) * HEAD)
        return jnp.concatenate([
            own_ref[:, at], near_one[:, at] + far_one[:, at], near_two[:, at] + far_two[:, at], far_three[:, at],
        ], axis=0)

    k, v = keys_of(0), keys_of(2 * HEAD)
    k_sum = jnp.zeros((HEAD, 4 * rows), F32)
    v_sum = jnp.zeros((HEAD, 4 * rows), F32)
    for first in range(0, 8, group):
        q = heads_of(q_ref, head * 8 + first, group, slice(None))
        g = heads_of(g_ref, head * 8 + first, group, slice(None))
        half, score_grad, out, q_grad = attend(q, g, k, v, bias)
        for j in range(group):
            at = slice((first + j) * HEAD, (first + j + 1) * HEAD)
            out_ref[:, at] = out[j * rows:(j + 1) * rows]
            qg_ref[:, at] = q_grad[j * rows:(j + 1) * rows]
        k_sum = k_sum + dot_tn(q, score_grad)
        v_sum = v_sum + dot_tn(g, half)
    k_grad = jnp.transpose(k_sum * SCALE).astype(BF16)
    v_grad = jnp.transpose(v_sum).astype(BF16)
    for i, ref in enumerate((own_o, one_o, two_o, three_o)):
        ref[:, :HEAD] = k_grad[i * rows:(i + 1) * rows]
        ref[:, HEAD:] = v_grad[i * rows:(i + 1) * rows]


def tile_work(q_ref, g_ref, k_ref, v_ref, labels, store):
    rows = 64
    seen = lax.broadcasted_iota(jnp.int32, (8, rows), 0).astype(F32)
    onehot = (seen == jnp.broadcast_to(labels, (8, rows))).astype(F32)
    same = dot_tn(onehot, onehot)
    col = lax.broadcasted_iota(jnp.int32, (rows, rows), 1)
    row = lax.broadcasted_iota(jnp.int32, (rows, rows), 0)
    bias = jnp.where((same > 0.5) & (col <= row), 0.0, MASKED).astype(F32)
    bias = jnp.concatenate([bias] * 8, axis=0)
    for h in range(2):
        ks = slice(h * HEAD, (h + 1) * HEAD)
        k, v = k_ref[:, ks], v_ref[:, ks]
        q = heads_of(q_ref, h * 8, 8, slice(None))
        g = heads_of(g_ref, h * 8, 8, slice(None))
        half, score_grad, out, q_grad = attend(q, g, k, v, bias)
        k_grad = (dot_tn(score_grad, q) * SCALE).astype(BF16)
        v_grad = dot_tn(half, g).astype(BF16)
        store(h, out, q_grad, k_grad, v_grad)


def store_tile(out_ref, qg_ref, kg_ref, vg_ref, h, out, q_grad, k_grad, v_grad):
    for j in range(8):
        at = slice((h * 8 + j) * HEAD, (h * 8 + j + 1) * HEAD)
        out_ref[0, :, at] = out[j * 64:(j + 1) * 64]
        qg_ref[0, :, at] = q_grad[j * 64:(j + 1) * 64]
    ks = slice(h * HEAD, (h + 1) * HEAD)
    kg_ref[0, :, ks] = k_grad
    vg_ref[0, :, ks] = v_grad


def kept_kernel(where_ref, q_ref, g_ref, k_ref, v_ref, seg_ref, out_ref, qg_ref, kg_ref, vg_ref):
    labels = seg_ref[pl.ds(where_ref[0, 0], 1), :].astype(F32)

    def store(*results):
        store_tile(out_ref, qg_ref, kg_ref, vg_ref, *results)

    tile_work(q_ref.at[0], g_ref.at[0], k_ref.at[0], v_ref.at[0], labels, store)


def moved_kernel(early_ref, late_ref, a, b, c, d, out_ref, qg_ref, kg_ref, vg_ref, pack_ref):
    pack_ref[...] = early_ref[...] + late_ref[...]
    labels = pack_ref[0:1, 4608:4672].astype(F32)

    def store(*results):
        store_tile(out_ref, qg_ref, kg_ref, vg_ref, *results)

    tile_work(
        pack_ref.at[:, 0:2048], pack_ref.at[:, 2048:4096], pack_ref.at[:, 4096:4352],
        pack_ref.at[:, 4352:4608], labels, store,
    )


def join(out_0, qg_0, out_1, qg_1, out_ref, qg_ref):
    for h, (out, qg) in enumerate(((out_0, qg_0), (out_1, qg_1))):
        at = slice(h * 8 * HEAD, (h + 1) * 8 * HEAD)
        out_ref[:, at] = out[...]
        qg_ref[:, at] = qg[...]


def finish(*refs):
    k_ref, v_ref = refs[-2:]
    for h in range(2):
        total = sum(ref[...].astype(F32) for ref in refs[4 * h:4 * h + 4])
        at = slice(h * HEAD, (h + 1) * HEAD)
        k_ref[:, at] = total[:, :HEAD].astype(BF16)
        v_ref[:, at] = total[:, HEAD:].astype(BF16)


def shaped(*shape):
    return jax.ShapeDtypeStruct(shape, BF16)


def cost(flops, moved, exps):
    return pl.CostEstimate(flops=flops, bytes_accessed=moved, transcendentals=exps)


def grant(mib):
    return pltpu.CompilerParams(vmem_limit_bytes=mib << 20)


def work(query_long, key_long, long_values, outgrad_long, query_short, key_short,
         short_values, outgrad_short, segments, assignment):
    rows = query_long.shape[1]
    size = lax.axis_size("ctx")
    whole = pl.BlockSpec(memory_space=pltpu.VMEM)
    packed = jnp.concatenate([key_long[0], long_values[0]], axis=1)
    last = size - 1
    near = [lax.ppermute(packed, "ctx", [(c, c + step) for c in range(last - step)]) for step in (1, 2)]
    far = [lax.ppermute(packed, "ctx", [(last - step, last)]) for step in (1, 2, 3)]

    short = (query_short[0], outgrad_short[0], key_short[0], short_values[0])
    widths = (2048, 2048, 256, 256)
    seg_spec = pl.BlockSpec((2, 64), lambda i, where: (0, 0))
    pack = pl.pallas_call(
        pack_tile,
        grid_spec=pltpu.PrefetchScalarGridSpec(
            num_scalar_prefetch=1, grid=(1,),
            in_specs=[pl.BlockSpec((1, 64, w), lambda i, where: (1 - where[0, 0], 0, 0)) for w in widths]
            + [seg_spec],
            out_specs=pl.BlockSpec((64, 4736), lambda i, where: (0, 0)),
        ),
        out_shape=shaped(64, 4736), name="pack_tile",
        cost_estimate=cost(0, 1 << 20, 0), compiler_params=grant(6),
    )(assignment, *short, segments[0])
    count = lax.axis_size("dp")
    pairs = [
        (source * size + c, (source + 1) % count * size + c) for source in range(count) for c in range(size)
    ]
    late = [((count - 1) * size, 0)]
    early = [pair for pair in pairs if pair not in late]
    arrived = lax.ppermute(pack, ("dp", "ctx"), early)
    arrived_late = lax.ppermute(pack, ("dp", "ctx"), late)

    tile_cost = cost(2 * 6 * 16 * 64 * 64 * 128, 1 << 20, 16 * 64 * 64)
    tile_shapes = [shaped(2, 64, w) for w in widths]
    kept = pl.pallas_call(
        kept_kernel,
        grid_spec=pltpu.PrefetchScalarGridSpec(
            num_scalar_prefetch=1, grid=(1,),
            in_specs=[pl.BlockSpec((1, 64, w), lambda i, where: (where[0, 0], 0, 0)) for w in widths]
            + [seg_spec],
            out_specs=[pl.BlockSpec((1, 64, w), lambda i, where: (0, 0, 0)) for w in widths],
        ),
        out_shape=tile_shapes, name="kept_tile",
        cost_estimate=tile_cost, compiler_params=grant(16),
    )(assignment, *short, segments[0])

    wide = []
    parts = []
    for h in range(2):
        results = pl.pallas_call(
            lambda *refs, h=h: long_head(*refs, head=h, group=GROUP),
            in_specs=[whole] * 8, out_specs=[whole] * 6,
            out_shape=[shaped(rows, 1024)] * 2 + [shaped(rows, 256)] * 4,
            cost_estimate=cost(6 * 8 * 128 * 512 * 128, 3 << 19, 8 * 128 * 512),
            compiler_params=grant(24),
        )(query_long[0], outgrad_long[0], packed, *near, *far)
        wide += results[:2]
        parts += [results[2]] + [
            lax.ppermute(part, "ctx", [(c, c - step) for c in range(step, size)])
            for step, part in zip((1, 2, 3), results[3:])
        ]
    done = pl.pallas_call(
        join, grid=(1,), in_specs=[whole] * 4,
        out_specs=[pl.BlockSpec((rows, 2048), lambda i: (0, 0))] * 2,
        out_shape=[shaped(rows, 2048)] * 2, name="join",
        cost_estimate=cost(0, 1 << 21, 0), compiler_params=grant(6),
    )(*wide)

    tiles = pl.pallas_call(
        moved_kernel,
        grid=(1,),
        in_specs=[whole] * 2
        + [pl.BlockSpec(memory_space=pl.ANY)] * 4,
        out_specs=[pl.BlockSpec((1, 64, w), lambda i: (1, 0, 0)) for w in widths],
        out_shape=tile_shapes, name="moved_tile",
        input_output_aliases={2: 0, 3: 1, 4: 2, 5: 3},
        scratch_shapes=[pltpu.VMEM((64, 4736), BF16)],
        cost_estimate=tile_cost, compiler_params=grant(16),
    )(arrived, arrived_late, *kept)

    key_sum, value_sum = pl.pallas_call(
        finish, out_shape=[shaped(rows, 256)] * 2, name="finish",
        cost_estimate=cost(1 << 18, 1 << 19, 0), compiler_params=grant(4),
    )(*parts)
    return (
        done[0][None], done[1][None], key_sum[None], value_sum[None],
        tiles[0][None], tiles[1][None], tiles[2][None], tiles[3][None],
    )


def solution(mesh):
    long_spec = P("dp", "ctx", "head")
    tile_spec = P("dp", "ctx", None, "head")
    return jax.shard_map(
        work, mesh=mesh,
        in_specs=(long_spec,) * 4 + (tile_spec,) * 4 + (P("dp", "ctx", None), P("dp", "ctx")),
        out_specs=(long_spec,) * 4 + (tile_spec,) * 4,
        check_vma=False,
    )
```
